128 devices in a mesh: fsdp: 16 (over y, z), seq: 8 (over x, core).
Axes of the slice: x: 4, y: 4, z: 4, core: 2. Of those that a mesh axis runs over, the one named last changes fastest.
Arguments:
- frames: bfloat16 [16, 3072, 1536], P('fsdp', 'seq'), may hold values from -0.59765625 to 0.59765625
- lengths: int32 [16, 12], P('fsdp'), may hold values from 1 to 512, 3072 in all within a row
- w_qkv: bfloat16 [1536, 3072], P('fsdp'), may hold values from -4 to 4
- d_context: bfloat16 [16, 3072, 1024], P('fsdp', 'seq'), may hold values from -0.59765625 to 0.59765625
Outputs:
- context: bfloat16 [16, 3072, 1024], P('fsdp', 'seq')
- grad_input: bfloat16 [16, 3072, 1536], P('fsdp', 'seq')
- grad_weight: float32 [1536, 3072], P('fsdp', 'seq')
The draws below stay inside these ranges and needn't reach their ends.
Inputs may be any that keep to these rules, and one draw needn't show every extreme that they name: The 12 lengths of a sequence sum to 3072, and the longest is exactly 512.
All inputs are finite; a program needn't handle non-finite values.
Results may differ from the reference program's by a relative error of at most 0.018.
Values may be sent and summed in bfloat16 or wider, within the bound.
A program may use at most 128 MiB of HBM per device.

```python
import math
import jax
import jax.numpy as jnp
import numpy as np
from jax import lax

D = 1536
HEADS = 16
HEAD_DIM = 64
MOST = 512
FRAMES = 3072
SEQS = 16
UTTS = 12


def draw_w_qkv(key, part):
    subkeys = jax.random.split(key, 4)
    inverse_root = 1.0 / math.sqrt(D)
    shape_heads = (D, HEADS, HEAD_DIM)
    query_part = jax.random.normal(subkeys[0], shape_heads, jnp.float32) * 1.5 * inverse_root
    key_part = jax.random.normal(subkeys[2], shape_heads, jnp.float32) * 1.5 * inverse_root
    value_part = jax.random.normal(subkeys[3], shape_heads, jnp.float32) * inverse_root
    width = HEADS * HEAD_DIM
    combined = jnp.concatenate([query_part.reshape(D, width), key_part.reshape(D, width), value_part.reshape(D, width)], axis=1)
    return jnp.clip(combined, -4.0, 4.0).astype(jnp.bfloat16)


def shard_levels(own_key, dims, cuts, least, top_value):
    level, own = 1.0, jax.random.fold_in(own_key, 6)
    for dim, parts in cuts:
        heights = jnp.exp(jax.random.uniform(jax.random.fold_in(own, dim), (parts,), jnp.float32, least / len(cuts), top_value / len(cuts)))
        level = level * jnp.repeat(heights, dims[dim] // parts).reshape([-1 if axis == dim else 1 for axis in range(len(dims))])
    return level


def split_up(count, total, reach, slope):
    loads = [(1 << 20) // math.isqrt(rank ** slope) + 1 for rank in range(2, count + 1)]
    rest, counts = total - reach - (count - 1), [1] * (count - 1)
    while rest > 0:
        free = [i for i in range(count - 1) if counts[i] < reach]
        mass, remaining = sum([loads[i] for i in free]), rest
        for i in free:
            extra = min(reach - counts[i], max(1, remaining * loads[i] // mass), rest)
            counts[i] = counts[i] + extra
            rest = rest - extra
    return np.array([reach] + counts)


def ragged_sizes(stream_key, count, total, bound, lean):
    if count == 2:
        one = jax.random.randint(stream_key, (), max(1, total - bound), min(bound, total - 1) + 1)
        return jnp.stack([one, total - one])
    sizes = jnp.asarray(split_up(count, total, bound, lean), jnp.int32)
    twos = (count - 1) // 2
    source_of, receiver = sizes[1:1 + 2 * twos:2], sizes[2:2 + 2 * twos:2]
    slack = jnp.minimum(source_of - 1, bound - receiver)
    shifted = jax.random.randint(jax.random.fold_in(stream_key, 1), (twos,), 0, 1 << 20) % (slack + 1)
    sizes = sizes.at[1:1 + 2 * twos:2].set(source_of - shifted).at[2:2 + 2 * twos:2].set(receiver + shifted)
    return sizes[jax.random.permutation(jax.random.fold_in(stream_key, 2), count)]


def scatter_about(own_key, extent, scale, bound, pieces=(), kind=jnp.bfloat16):
    drawn = jax.random.normal(own_key, extent, jnp.float32) * scale
    if len(pieces) > 0:
        drawn = shard_levels(own_key, extent, pieces, -0.22, 0.18) * drawn
    return jnp.clip(drawn, min=-bound, max=bound).astype(kind)


def setup_inputs(seed: int = 0) -> dict:
    key_list = jax.random.split(jax.random.key(seed), 5)
    return {
        "frames": scatter_about(key_list[0], (SEQS, FRAMES, D), 0.1, 0.59765625, ((0, 16), (1, 8))),
        "lengths": jax.vmap(lambda own: ragged_sizes(own, UTTS, FRAMES, MOST, 2))(jax.random.split(key_list[1], SEQS)).reshape((SEQS, UTTS)).astype(jnp.int32),
        "w_qkv": draw_w_qkv(jax.random.fold_in(key_list[4], 71), 0),
        "d_context": scatter_about(key_list[3], (SEQS, FRAMES, HEADS * HEAD_DIM), 0.1, 0.59765625, ((0, 16), (1, 8))),
    }


def segment_ids(lengths, frame_total):
    utter_ends = jnp.cumsum(lengths).astype(jnp.int32)
    positions = jnp.arange(frame_total, dtype=jnp.int32)
    return lax.optimization_barrier(jnp.sum((positions[:, None] >= utter_ends[None, :]).astype(jnp.int32), axis=1)).astype(jnp.int32)

def attend(query, keys, values, grad_out, segment):
    frame_total = query.shape[0]
    block_rows = 512 if frame_total % 512 == 0 and frame_total >= 512 else frame_total
    key_span = min(block_rows + 2 * MOST, frame_total)
    block_count = frame_total // block_rows
    score_scale = HEAD_DIM ** (-0.5)

    def block_step(block_index, state_tuple):
        context, grad_query, grad_key, grad_value = state_tuple
        block_start = (block_index * block_rows).astype(jnp.int32)
        anchor = jnp.clip(block_start - MOST, 0, frame_total - key_span).astype(jnp.int32)
        query_block = lax.dynamic_slice_in_dim(query, block_start, block_rows, 0).astype(jnp.float32)
        grad_block = lax.dynamic_slice_in_dim(grad_out, block_start, block_rows, 0).astype(jnp.float32)
        segment_query = lax.dynamic_slice_in_dim(segment, block_start, block_rows, 0)
        key_window = lax.dynamic_slice_in_dim(keys, anchor, key_span, 0).astype(jnp.float32)
        value_window = lax.dynamic_slice_in_dim(values, anchor, key_span, 0).astype(jnp.float32)
        segment_key = lax.dynamic_slice_in_dim(segment, anchor, key_span, 0)
        scores = jnp.einsum('qhd,khd->hqk', query_block, key_window) * score_scale
        same_utterance = segment_query[:, None] == segment_key[None, :]
        scores = jnp.where(same_utterance[None], scores, -jnp.inf)
        row_max = lax.optimization_barrier(jnp.max(scores, axis=-1, keepdims=True))
        exponent = jnp.exp(scores - row_max)
        softmax_out = exponent / lax.optimization_barrier(jnp.sum(exponent, axis=-1, keepdims=True))
        weights = softmax_out.astype(jnp.bfloat16).astype(jnp.float32)
        out_block = jnp.einsum('hqk,khd->qhd', weights, value_window).astype(jnp.bfloat16)
        value_term = jnp.einsum('hqk,qhd->khd', weights, grad_block)
        dprobs = jnp.einsum('qhd,khd->hqk', grad_block, value_window)
        dscores = softmax_out * (dprobs - lax.optimization_barrier(jnp.sum(softmax_out * dprobs, axis=-1, keepdims=True))) * score_scale
        dscores = dscores.astype(jnp.bfloat16).astype(jnp.float32)
        query_term = jnp.einsum('hqk,khd->qhd', dscores, key_window).astype(jnp.bfloat16)
        key_term = jnp.einsum('hqk,qhd->khd', dscores, query_block)
        context = lax.dynamic_update_slice_in_dim(context, out_block, block_start, 0)
        grad_query = lax.dynamic_update_slice_in_dim(grad_query, query_term, block_start, 0)
        grad_key = lax.dynamic_update_slice_in_dim(grad_key, lax.dynamic_slice_in_dim(grad_key, anchor, key_span, 0) + key_term, anchor, 0)
        grad_value = lax.dynamic_update_slice_in_dim(grad_value, lax.dynamic_slice_in_dim(grad_value, anchor, key_span, 0) + value_term, anchor, 0)
        return (context, grad_query, grad_key, grad_value)
    shape_one = query.shape
    initial = (jnp.zeros(shape_one, jnp.bfloat16), jnp.zeros(shape_one, jnp.bfloat16), jnp.zeros(shape_one, jnp.float32), jnp.zeros(shape_one, jnp.float32))
    context, grad_query, grad_key, grad_value = lax.fori_loop(0, block_count, block_step, initial)
    return (context, grad_query, grad_key.astype(jnp.bfloat16), grad_value.astype(jnp.bfloat16))

def reference(frames, lengths, w_qkv, d_context):
    width = HEADS * HEAD_DIM
    weight_full = w_qkv.astype(jnp.float32)

    def per_sequence(grad_sum, sequence_item):
        activations, utter_lengths, cotangent = sequence_item
        values_in = activations.astype(jnp.float32)
        average = lax.optimization_barrier(jnp.mean(values_in, axis=1, keepdims=True))
        centred = values_in - average
        variance = lax.optimization_barrier(jnp.mean(centred * centred, axis=1, keepdims=True))
        inverse_scale = lax.rsqrt(variance + 1e-05)
        whitened = centred * inverse_scale
        normed = whitened.astype(jnp.bfloat16)
        qkv = jnp.dot(normed.astype(jnp.float32), weight_full, preferred_element_type=jnp.float32)
        qkv = qkv.astype(jnp.bfloat16).reshape(FRAMES, 3, HEADS, HEAD_DIM)
        segment = segment_ids(utter_lengths, FRAMES)
        context, grad_query, grad_key, grad_value = attend(qkv[:, 0], qkv[:, 1], qkv[:, 2], cotangent.reshape(FRAMES, HEADS, HEAD_DIM), segment)
        grad_qkv = jnp.stack([grad_query, grad_key, grad_value], axis=1).reshape(FRAMES, 3 * width)
        grad_qkv_f = grad_qkv.astype(jnp.float32)
        grad_normed = jnp.dot(grad_qkv_f, weight_full.T, preferred_element_type=jnp.float32)
        grad_input = inverse_scale * (grad_normed - lax.optimization_barrier(jnp.mean(grad_normed, axis=1, keepdims=True)) - whitened * lax.optimization_barrier(jnp.mean(grad_normed * whitened, axis=1, keepdims=True)))
        grad_sum = grad_sum + jnp.dot(normed.astype(jnp.float32).T, grad_qkv_f, preferred_element_type=jnp.float32)
        return (grad_sum, (context.reshape(FRAMES, width), grad_input.astype(jnp.bfloat16)))
    grad_weight, (context, grad_input) = lax.scan(per_sequence, jnp.zeros((D, 3 * width), jnp.float32), (frames, lengths, d_context))
    return (context, grad_input, grad_weight)
```

```python
import functools

import jax
import jax.numpy as jnp
from jax import lax
from jax.experimental import pallas as pl
from jax.experimental.pallas import tpu as pltpu
from jax.sharding import PartitionSpec as P

LOG2E = 1.4426950408889634
NT = (((1,), (1,)), ((), ()))
TN = (((0,), (0,)), ((), ()))


def attend_body(total, unroll, len_ref, qkv_ref, do_ref, ctx_ref, grad_ref, gk_t, gv_t):
    lane = lax.broadcasted_iota(jnp.int32, (128, 128), 1)
    low = lane < 64

    def twice(x):
        zero = jnp.zeros_like(x)
        return jnp.concatenate([jnp.where(low, x, zero), jnp.where(low, zero, x)], axis=0)

    def fold(x):
        return jnp.where(low, x[:128], x[128:])

    def window(span, start, end):
        base = pl.multiple_of(jnp.minimum((start // 16) * 16, total - span), 16)
        key_pos = base + lax.broadcasted_iota(jnp.int32, (1, span), 1)
        bias = jnp.where((key_pos >= start) & (key_pos < end), 0.0, -1e30).astype(jnp.float32)
        gk_t[:, :span] = jnp.zeros((128, span), jnp.float32)
        gv_t[:, :span] = jnp.zeros((128, span), jnp.float32)

        def block(index, _):
            row = pl.multiple_of(base + index * 128, 16)
            rows = pl.ds(row, 128)
            keys = qkv_ref[pl.ds(base, span), 128:256]
            values = qkv_ref[pl.ds(base, span), 256:384]
            row_pos = row + lax.broadcasted_iota(jnp.int32, (128, 128), 0)
            valid = (row_pos >= start) & (row_pos < end)
            query = twice(qkv_ref[rows, 0:128])
            cot = jnp.where(valid, do_ref[rows, :].astype(jnp.float32), 0.0)
            cot = twice(cot)
            s = lax.dot_general(query, keys, NT, preferred_element_type=jnp.float32)
            s = s * (0.125 * LOG2E) + bias
            e = jnp.exp2(s - jnp.max(s, axis=1, keepdims=True))
            inv = 1.0 / jnp.sum(e, axis=1, keepdims=True)
            weights = e.astype(jnp.bfloat16)
            ctx = jnp.dot(weights, values, preferred_element_type=jnp.float32) * inv
            cot_n = cot * inv
            delta = jnp.sum(cot_n * ctx, axis=1, keepdims=True)
            cot_b = cot_n.astype(jnp.bfloat16)
            dp = lax.dot_general(cot_b, values, NT, preferred_element_type=jnp.float32)
            ds = (e * (dp - delta)).astype(jnp.bfloat16)
            gv_t[:, :span] += lax.dot_general(cot_b, weights, TN, preferred_element_type=jnp.float32)
            gk_t[:, :span] += lax.dot_general(query, ds, TN, preferred_element_type=jnp.float32)
            gq = jnp.dot(ds, keys, preferred_element_type=jnp.float32)
            ctx_ref[rows, :] = jnp.where(valid, fold(ctx), ctx_ref[rows, :].astype(jnp.float32)).astype(jnp.bfloat16)
            grad_ref[rows, 0:128] = jnp.where(
                valid, fold(gq) * 0.125, grad_ref[rows, 0:128].astype(jnp.float32)).astype(jnp.bfloat16)
            return 0

        lax.fori_loop(0, span // 128, block, 0, unroll=min(unroll, span // 128) if unroll else True)
        for part in range(span // 128):
            rows = pl.ds(pl.multiple_of(base + part * 128, 16), 128)
            row_pos = base + part * 128 + lax.broadcasted_iota(jnp.int32, (128, 128), 0)
            valid = (row_pos >= start) & (row_pos < end)
            cols = slice(part * 128, part * 128 + 128)
            gk = gk_t[:, cols].T * 0.125
            gv = gv_t[:, cols].T
            grad_ref[rows, 128:256] = jnp.where(
                valid, gk, grad_ref[rows, 128:256].astype(jnp.float32)).astype(jnp.bfloat16)
            grad_ref[rows, 256:384] = jnp.where(
                valid, gv, grad_ref[rows, 256:384].astype(jnp.float32)).astype(jnp.bfloat16)

    def utterance(index, start):
        end = start + len_ref[index]
        tiles = (end - (start // 16) * 16 + 127) // 128
        for count in range(1, 6):
            @pl.when(tiles == count)
            def _():
                window(count * 128, start, end)
        return end

    lax.fori_loop(0, len_ref.shape[0], utterance, jnp.int32(0))


def attend(lengths, qkv, cot, unroll=1):
    total = qkv.shape[0]
    return pl.pallas_call(
        functools.partial(attend_body, total, unroll),
        out_shape=(jax.ShapeDtypeStruct((total, 128), jnp.bfloat16),
                   jax.ShapeDtypeStruct((total, 384), jnp.bfloat16)),
        in_specs=[pl.BlockSpec(memory_space=pltpu.SMEM)] + [pl.BlockSpec(memory_space=pltpu.VMEM)] * 2,
        out_specs=(pl.BlockSpec(memory_space=pltpu.VMEM),) * 2,
        scratch_shapes=[pltpu.VMEM((128, 640), jnp.float32)] * 2,
        name="attention",
    )(lengths, qkv, cot)


def per_device(frames, lengths, w_qkv, d_context):
    values_in = frames[0].astype(jnp.float32)
    frame_count, model = values_in.shape
    ranks = lax.axis_size("seq")
    rank = lax.axis_index("seq")
    total = frame_count * ranks
    width = d_context.shape[2]
    per_rank = width // ranks
    average = jnp.mean(values_in, axis=1, keepdims=True)
    centred = values_in - average
    variance = jnp.mean(centred * centred, axis=1, keepdims=True)
    inverse_scale = lax.rsqrt(variance + 1e-05)
    whitened = centred * inverse_scale
    normed = whitened.astype(jnp.bfloat16)
    rows = w_qkv.shape[0]
    own = lax.dynamic_slice_in_dim(w_qkv.reshape(rows, 3, width), rank * per_rank, per_rank, 2)
    own_full = lax.all_gather(own.reshape(rows, 3 * per_rank), "fsdp", axis=0, tiled=True)
    cot = lax.all_to_all(
        d_context[0].reshape(frame_count, ranks, per_rank).transpose(1, 0, 2), "seq", 0, 0, tiled=True
    ).reshape(total, per_rank)
    normed_full = lax.all_gather(normed, "seq", axis=0, tiled=True)
    weight_full = lax.all_gather(w_qkv, "fsdp", axis=0, tiled=True)
    qkv = jnp.dot(normed_full, own_full, preferred_element_type=jnp.float32).astype(jnp.bfloat16)
    context, grads = attend(lengths[0], qkv, cot, 5)
    context_back = lax.all_to_all(context.reshape(ranks, frame_count, per_rank), "seq", 0, 0, tiled=True)
    grads_back = lax.all_to_all(grads.reshape(ranks, frame_count, 3 * per_rank), "seq", 0, 0, tiled=True)
    partial = lax.dot_general(
        normed_full, grads, (((0,), (0,)), ((), ())), preferred_element_type=jnp.float32
    ).astype(jnp.bfloat16)
    owned = lax.psum_scatter(partial, "fsdp", scatter_dimension=0, tiled=True)
    blocks = lax.all_gather(owned.reshape(rows, 3, per_rank), "seq", axis=2, tiled=True)
    grad_weight = lax.dynamic_slice_in_dim(
        blocks.reshape(rows, 3 * width), rank * 3 * per_rank, 3 * per_rank, 1
    ).astype(jnp.float32)
    context_out = context_back.transpose(1, 0, 2).reshape(1, frame_count, width)
    grad_qkv = (
        grads_back.reshape(ranks, frame_count, 3, per_rank).transpose(1, 2, 0, 3).reshape(frame_count, 3 * width)
    )
    grad_normed = lax.dot_general(
        grad_qkv, weight_full, (((1,), (1,)), ((), ())), preferred_element_type=jnp.float32
    )
    grad_input = inverse_scale * (
        grad_normed
        - jnp.mean(grad_normed, axis=1, keepdims=True)
        - whitened * jnp.mean(grad_normed * whitened, axis=1, keepdims=True)
    )
    return context_out, grad_input.astype(jnp.bfloat16)[None], grad_weight


def solution(mesh):
    return jax.shard_map(
        per_device,
        mesh=mesh,
        in_specs=(P("fsdp", "seq", None), P("fsdp", None), P("fsdp", None), P("fsdp", "seq", None)),
        out_specs=(P("fsdp", "seq", None), P("fsdp", "seq", None), P("fsdp", "seq")),
        check_vma=False,
    )
```

```python
import functools

import jax
import jax.numpy as jnp
from jax import lax
from jax.experimental import pallas as pl
from jax.experimental.pallas import tpu as pltpu
from jax.sharding import PartitionSpec as P

LOG2E = 1.4426950408889634
NT = (((1,), (1,)), ((), ()))
TN = (((0,), (0,)), ((), ()))


def attend_body(total, unroll, len_ref, qkv_ref, do_ref, ctx_ref, grad_ref, gk_t, gv_t):
    lane = lax.broadcasted_iota(jnp.int32, (128, 128), 1)
    low = lane < 64

    def twice(x):
        zero = jnp.zeros_like(x)
        return jnp.concatenate([jnp.where(low, x, zero), jnp.where(low, zero, x)], axis=0)

    def fold(x):
        return jnp.where(low, x[:128], x[128:])

    def window(span, start, end):
        base = pl.multiple_of(jnp.minimum((start // 16) * 16, total - span), 16)
        key_pos = base + lax.broadcasted_iota(jnp.int32, (1, span), 1)
        bias = jnp.where((key_pos >= start) & (key_pos < end), 0.0, -1e30).astype(jnp.float32)
        gk_t[:, :span] = jnp.zeros((128, span), jnp.float32)
        gv_t[:, :span] = jnp.zeros((128, span), jnp.float32)

        def block(index, _):
            row = pl.multiple_of(base + index * 128, 16)
            rows = pl.ds(row, 128)
            keys = qkv_ref[pl.ds(base, span), 128:256]
            values = qkv_ref[pl.ds(base, span), 256:384]
            row_pos = row + lax.broadcasted_iota(jnp.int32, (128, 128), 0)
            valid = (row_pos >= start) & (row_pos < end)
            query = twice(qkv_ref[rows, 0:128])
            cot = jnp.where(valid, do_ref[rows, :].astype(jnp.float32), 0.0)
            cot = twice(cot)
            s = lax.dot_general(query, keys, NT, preferred_element_type=jnp.float32)
            s = s * (0.125 * LOG2E) + bias
            e = jnp.exp2(s - jnp.max(s, axis=1, keepdims=True))
            inv = 1.0 / jnp.sum(e, axis=1, keepdims=True)
            weights = e.astype(jnp.bfloat16)
            ctx = jnp.dot(weights, values, preferred_element_type=jnp.float32) * inv
            cot_n = cot * inv
            delta = jnp.sum(cot_n * ctx, axis=1, keepdims=True)
            cot_b = cot_n.astype(jnp.bfloat16)
            dp = lax.dot_general(cot_b, values, NT, preferred_element_type=jnp.float32)
            ds = (e * (dp - delta)).astype(jnp.bfloat16)
            gv_t[:, :span] += lax.dot_general(cot_b, weights, TN, preferred_element_type=jnp.float32)
            gk_t[:, :span] += lax.dot_general(query, ds, TN, preferred_element_type=jnp.float32)
            gq = jnp.dot(ds, keys, preferred_element_type=jnp.float32)
            ctx_ref[rows, :] = jnp.where(valid, fold(ctx), ctx_ref[rows, :].astype(jnp.float32)).astype(jnp.bfloat16)
            grad_ref[rows, 0:128] = jnp.where(
                valid, fold(gq) * 0.125, grad_ref[rows, 0:128].astype(jnp.float32)).astype(jnp.bfloat16)
            return 0

        lax.fori_loop(0, span // 128, block, 0, unroll=min(unroll, span // 128) if unroll else True)
        for part in range(span // 128):
            rows = pl.ds(pl.multiple_of(base + part * 128, 16), 128)
            row_pos = base + part * 128 + lax.broadcasted_iota(jnp.int32, (128, 128), 0)
            valid = (row_pos >= start) & (row_pos < end)
            cols = slice(part * 128, part * 128 + 128)
            gk = gk_t[:, cols].T * 0.125
            gv = gv_t[:, cols].T
            grad_ref[rows, 128:256] = jnp.where(
                valid, gk, grad_ref[rows, 128:256].astype(jnp.float32)).astype(jnp.bfloat16)
            grad_ref[rows, 256:384] = jnp.where(
                valid, gv, grad_ref[rows, 256:384].astype(jnp.float32)).astype(jnp.bfloat16)

    def utterance(index, start):
        end = start + len_ref[index]
        tiles = (end - (start // 16) * 16 + 127) // 128
        for count in range(1, 6):
            @pl.when(tiles == count)
            def _():
                window(count * 128, start, end)
        return end

    lax.fori_loop(0, len_ref.shape[0], utterance, jnp.int32(0))


def attend(lengths, qkv, cot, unroll=1):
    total = qkv.shape[0]
    return pl.pallas_call(
        functools.partial(attend_body, total, unroll),
        out_shape=(jax.ShapeDtypeStruct((total, 128), jnp.bfloat16),
                   jax.ShapeDtypeStruct((total, 384), jnp.bfloat16)),
        in_specs=[pl.BlockSpec(memory_space=pltpu.SMEM)] + [pl.BlockSpec(memory_space=pltpu.VMEM)] * 2,
        out_specs=(pl.BlockSpec(memory_space=pltpu.VMEM),) * 2,
        scratch_shapes=[pltpu.VMEM((128, 640), jnp.float32)] * 2,
        name="attention",
    )(lengths, qkv, cot)


MESH = pl.DeviceIdType.MESH
BF = jnp.bfloat16
F32 = jnp.float32


def place():
    f = lax.axis_index("fsdp")
    s = lax.axis_index("seq")
    return f, s


def greet(f, s, ranks, shards):
    barrier = pltpu.get_barrier_semaphore()
    for k in range(1, ranks):
        pl.semaphore_signal(barrier, inc=1, device_id=(f, lax.rem(s + k, ranks)), device_id_type=MESH)
    for k in range(1, shards):
        pl.semaphore_signal(barrier, inc=1, device_id=(lax.rem(f + k, shards), s), device_id_type=MESH)
    pl.semaphore_wait(barrier, ranks + shards - 2)


def whiten(values_in):
    average = jnp.mean(values_in, axis=1, keepdims=True)
    centred = values_in - average
    variance = jnp.mean(centred * centred, axis=1, keepdims=True)
    inverse_scale = lax.rsqrt(variance + 1e-05)
    return centred * inverse_scale, inverse_scale


def front_body(ranks, shards, frames, cot_in, w_in, normed, qkv, cot, w_own, stage,
               cot_send, cot_recv, w_send, w_recv, send, recv, local):
    f, s = place()
    rows = frames.shape[0]
    half = rows // 2
    chip, core = s // 2, lax.rem(s, 2)
    chips = ranks // 2
    right = lax.rem(chip + 1, chips) * 2 + core
    left = lax.rem(chip + chips - 1, chips) * 2 + core
    across = lax.rem(chip + 2, chips) * 2 + core
    flip = 1 - 2 * core
    partner = s + flip
    depth = w_in.shape[0]
    head = pl.ds(pl.multiple_of(s * 128, 128), 128)

    parts = []
    for t in range(3):
        column = pl.multiple_of(t * ranks * 128 + s * 128, 128)
        parts.append(pltpu.make_async_copy(w_in.at[:, pl.ds(column, 128)], stage.at[:, pl.ds(t * 128, 128)], local.at[t]))
        parts[t].start()
    greet(f, s, ranks, shards)

    def block(rank, offset=0, count=rows):
        return normed.at[pl.ds(pl.multiple_of(rank * rows + offset, 64), count)]

    def move(role, rank, offset, count, target):
        copy = pltpu.make_async_remote_copy(
            src_ref=block(rank, offset, count), dst_ref=block(rank, offset, count),
            send_sem=send.at[role], recv_sem=recv.at[role], device_id=(f, target), device_id_type=MESH)
        copy.start()
        started.append(copy)

    def arrived(role, rank, offset, count):
        pltpu.make_async_remote_copy(
            src_ref=block(rank, offset, count), dst_ref=block(rank, offset, count),
            send_sem=send.at[role], recv_sem=recv.at[role], device_id=(f, s), device_id_type=MESH).wait_recv()

    started = []
    cots = []
    for k in (4, 3, 5, 2, 6, 1, 7):
        d = lax.rem(s + k, ranks)
        copy = pltpu.make_async_remote_copy(
            src_ref=cot_in.at[:, pl.ds(pl.multiple_of(d * 128, 128), 128)],
            dst_ref=cot.at[pl.ds(pl.multiple_of(s * rows, 128), rows)],
            send_sem=cot_send.at[k], recv_sem=cot_recv.at[k], device_id=(f, d), device_id_type=MESH)
        copy.start()
        cots.append(copy)
    for part in parts:
        part.wait()
    slices = []
    for k in range(1, shards):
        copy = pltpu.make_async_remote_copy(
            src_ref=stage, dst_ref=w_own.at[pl.ds(pl.multiple_of(f * depth, 32), depth)],
            send_sem=w_send.at[k], recv_sem=w_recv.at[k],
            device_id=(lax.rem(f + k, shards), s), device_id_type=MESH)
        copy.start()
        slices.append(copy)

    def norm(offset):
        whitened, _ = whiten(frames[pl.ds(offset, half), :].astype(F32))
        normed[pl.ds(pl.multiple_of(s * rows + offset, 64), half), :] = whitened.astype(BF)

    norm(0)
    move(0, s, 0, half, right)
    norm(half)
    move(2, s, half, half, left)
    move(1, s, half, half, right)
    move(3, s, 0, half, left)
    move(6, s, 0, rows, partner)
    cot[pl.ds(pl.multiple_of(s * rows, 128), rows), :] = cot_in[:, head]
    w_own[pl.ds(pl.multiple_of(f * depth, 32), depth), :] = stage[...]

    arrived(0, left, 0, half)
    move(4, left, 0, half, right)
    arrived(2, right, half, half)
    move(5, right, half, half, left)

    def project(rank):
        def tile(i, _):
            at = pl.ds(pl.multiple_of(rank * rows + i * half, 64), half)
            qkv[at, :] = jnp.dot(normed[at, :], w_own[...], preferred_element_type=F32).astype(BF)
            return 0
        lax.fori_loop(0, 2, tile, 0)

    for k in range(1, shards):
        slices[k - 1].wait_recv()
    project(s)
    arrived(6, partner, 0, rows)
    project(partner)
    arrived(1, left, half, half)
    move(7, left, 0, rows, partner)
    arrived(3, right, 0, half)
    move(8, right, 0, rows, partner)
    project(left)
    project(right)
    arrived(7, left + flip, 0, rows)
    project(left + flip)
    arrived(8, right + flip, 0, rows)
    project(right + flip)
    arrived(4, across, 0, half)
    move(9, across, 0, half, partner)
    arrived(5, across, half, half)
    move(10, across, half, half, partner)
    project(across)
    arrived(9, across + flip, 0, half)
    arrived(10, across + flip, half, half)
    project(across + flip)
    for copy in cots:
        copy.wait()
    for copy in slices + started:
        copy.wait_send()


VM = pl.BlockSpec(memory_space=pltpu.VMEM)
ANY = pl.BlockSpec(memory_space=pl.ANY)
DMA = pltpu.SemaphoreType.DMA


def front(ranks, shards, frames, cot_in, w_in):
    rows, model = frames.shape
    total = rows * ranks
    return pl.pallas_call(
        functools.partial(front_body, ranks, shards),
        out_shape=(jax.ShapeDtypeStruct((total, model), BF), jax.ShapeDtypeStruct((total, 384), BF),
                   jax.ShapeDtypeStruct((total, 128), BF)),
        in_specs=[VM] * 3,
        out_specs=(VM,) * 3,
        scratch_shapes=[pltpu.VMEM((model, 384), BF), pltpu.VMEM((model // shards, 384), BF),
                        DMA((ranks,)), DMA((ranks,)), DMA((shards,)), DMA((shards,)), DMA((11,)), DMA((11,)), DMA((3,))],
        compiler_params=pltpu.CompilerParams(collective_id=0, has_side_effects=True, vmem_limit_bytes=40 * 2**20),
        name="front",
    )(frames, cot_in, w_in)


def back_body(ranks, shards, ctx, grads, frames, normed_in, w_in, ctx_out, gi_out, gw_out,
              normed, w, grads_t, got, part, shares, acc, white, scale, total_w,
              g_send, g_recv, c_send, c_recv, r_send, r_recv, p_send, p_recv, local):
    f, s = place()
    rows, model = frames.shape
    depth = model // shards
    sides = 4
    fy, fz = f // sides, lax.rem(f, sides)
    load_n = pltpu.make_async_copy(normed_in, normed, local.at[0])
    load_w = pltpu.make_async_copy(w_in, w, local.at[1])
    load_n.start()
    load_w.start()
    greet(f, s, ranks, shards)
    order = (1, 7, 2, 6, 3, 5, 4)
    sent = {}
    for k in order:
        d = lax.rem(s + k, ranks)
        theirs = pl.ds(pl.multiple_of(d * rows, 128), rows)
        sent[k] = (
            pltpu.make_async_remote_copy(
                src_ref=grads.at[theirs], dst_ref=got.at[k], send_sem=g_send.at[k], recv_sem=g_recv.at[k],
                device_id=(f, d), device_id_type=MESH),
            pltpu.make_async_remote_copy(
                src_ref=ctx.at[theirs], dst_ref=ctx_out.at[:, pl.ds(pl.multiple_of(s * 128, 128), 128)],
                send_sem=c_send.at[k], recv_sem=c_recv.at[k], device_id=(f, d), device_id_type=MESH))
        for copy in sent[k]:
            copy.start()
    mine = pl.ds(pl.multiple_of(s * rows, 128), rows)
    ctx_out[:, pl.ds(pl.multiple_of(s * 128, 128), 128)] = ctx[mine, :]

    def turn(i, _):
        at = pl.ds(pl.multiple_of(i * 128, 128), 128)
        grads_t[:, at] = grads[at, :].T
        return 0

    lax.fori_loop(0, grads.shape[0] // 128, turn, 0)
    load_n.wait()
    group = depth * sides
    shared = []
    for j in (1, 2, 3, 0):
        y = lax.rem(fy + j, sides)
        at = pl.ds(pl.multiple_of(y * group, 128), group)
        product = jnp.dot(grads_t[...], normed[:, at], preferred_element_type=F32)
        part[at, :] = product.T.astype(BF)
        for k in (1, 2, 3, 0):
            if j == 0 and k == 0:
                continue
            peer = y * sides + lax.rem(fz + k, sides)
            copy = pltpu.make_async_remote_copy(
                src_ref=part.at[pl.ds(pl.multiple_of(peer * depth, 32), depth)], dst_ref=shares.at[4 * j + k],
                send_sem=r_send.at[4 * j + k], recv_sem=r_recv.at[4 * j + k],
                device_id=(peer, s), device_id_type=MESH)
            copy.start()
            shared.append(copy)

    def prepare(i, _):
        at = pl.ds(pl.multiple_of(i * depth, 32), depth)
        whitened, inverse_scale = whiten(frames[at, :].astype(F32))
        white[at, :] = whitened
        scale[at, :] = jnp.broadcast_to(inverse_scale, (depth, 128))
        return 0

    lax.fori_loop(0, rows // depth, prepare, 0)
    load_w.wait()

    def pull(block, rank):
        return lax.dot_general(block, w[rank], NT, preferred_element_type=F32)

    acc[...] = pull(grads[mine, :], s)
    for k in order[:4]:
        sent[k][0].wait_recv()
        acc[...] += pull(got[k], lax.rem(s + ranks - k, ranks))
    for copy in shared:
        copy.wait_recv()
    sums = part[pl.ds(pl.multiple_of(f * depth, 32), depth), :].astype(F32)
    for k in range(1, shards):
        sums += shares[k].astype(F32)
    total_w[...] = sums
    for t in range(3):
        number = t * ranks + s
        owner, slot = number // 3, lax.rem(number, 3)
        source = total_w.at[:, pl.ds(t * 128, 128)]
        target = gw_out.at[:, pl.ds(pl.multiple_of(slot * 128, 128), 128)]

        @pl.when(owner != s)
        def _():
            pltpu.make_async_remote_copy(
                src_ref=source, dst_ref=target, send_sem=p_send.at[t], recv_sem=p_recv.at[slot],
                device_id=(f, owner), device_id_type=MESH).start()

        @pl.when(owner == s)
        def _():
            target[...] = sums[:, t * 128:t * 128 + 128]

    for k in order[4:]:
        sent[k][0].wait_recv()
        acc[...] += pull(got[k], lax.rem(s + ranks - k, ranks))

    def finish(i, _):
        at = pl.ds(pl.multiple_of(i * depth, 32), depth)
        gn = acc[at, :]
        whitened = white[at, :]
        inner = jnp.mean(gn * whitened, axis=1, keepdims=True)
        out = scale[at, 0:1] * (gn - jnp.mean(gn, axis=1, keepdims=True) - whitened * inner)
        gi_out[at, :] = out.astype(BF)
        return 0

    lax.fori_loop(0, rows // depth, finish, 0)
    for slot in range(3):
        source_rank = lax.rem(3 * s + slot, ranks)

        @pl.when(source_rank != s)
        def _():
            pltpu.make_async_remote_copy(
                src_ref=total_w.at[:, pl.ds(0, 128)], dst_ref=gw_out.at[:, pl.ds(slot * 128, 128)],
                send_sem=p_send.at[slot], recv_sem=p_recv.at[slot], device_id=(f, s), device_id_type=MESH).wait_recv()

    for t in range(3):
        owner = (t * ranks + s) // 3

        @pl.when(owner != s)
        def _():
            pltpu.make_async_remote_copy(
                src_ref=total_w.at[:, pl.ds(t * 128, 128)], dst_ref=gw_out.at[:, pl.ds(0, 128)],
                send_sem=p_send.at[t], recv_sem=p_recv.at[t], device_id=(f, owner), device_id_type=MESH).wait_send()

    for k in order:
        sent[k][0].wait_send()
        sent[k][1].wait()
    for copy in shared:
        copy.wait_send()


def back(ranks, shards, ctx, grads, frames, normed, w):
    rows, model = frames.shape
    total = rows * ranks
    depth = model // shards
    return pl.pallas_call(
        functools.partial(back_body, ranks, shards),
        out_shape=(jax.ShapeDtypeStruct((rows, ranks * 128), BF), jax.ShapeDtypeStruct((rows, model), BF),
                   jax.ShapeDtypeStruct((depth, 384), F32)),
        in_specs=[VM] * 3 + [ANY] * 2,
        out_specs=(VM,) * 3,
        scratch_shapes=[
            pltpu.VMEM((total, model), BF), pltpu.VMEM((ranks, model, 384), BF), pltpu.VMEM((384, total), BF),
            pltpu.VMEM((ranks, rows, 384), BF), pltpu.VMEM((model, 384), BF), pltpu.VMEM((shards, depth, 384), BF),
            pltpu.VMEM((rows, model), F32), pltpu.VMEM((rows, model), F32), pltpu.VMEM((rows, 128), F32),
            pltpu.VMEM((depth, 384), F32)]
        + [DMA((ranks,))] * 4 + [DMA((shards,))] * 2 + [DMA((3,))] * 2 + [DMA((2,))],
        compiler_params=pltpu.CompilerParams(collective_id=1, has_side_effects=True, vmem_limit_bytes=60 * 2**20),
        name="back",
    )(ctx, grads, frames, normed, w)


def per_device(frames, lengths, w_qkv, d_context):
    ranks, shards = lax.axis_size("seq"), lax.axis_size("fsdp")
    depth, model = w_qkv.shape[0], frames.shape[2]
    by_owner = w_qkv.reshape(depth, 3, ranks, 128).transpose(2, 0, 1, 3).reshape(ranks, depth, 384)
    weight_full = lax.all_gather(by_owner, "fsdp", axis=1, tiled=True)
    normed, qkv, cot = front(ranks, shards, frames[0], d_context[0], w_qkv)
    context, grads = attend(lengths[0], qkv, cot, 5)
    context_out, grad_input, grad_weight = back(ranks, shards, context, grads, frames[0], normed, weight_full)
    return context_out[None], grad_input[None], grad_weight


def solution(mesh):
    return jax.shard_map(
        per_device,
        mesh=mesh,
        in_specs=(P("fsdp", "seq", None), P("fsdp", None), P("fsdp", None), P("fsdp", "seq", None)),
        out_specs=(P("fsdp", "seq", None), P("fsdp", "seq", None), P("fsdp", "seq")),
        check_vma=False,
    )
```

```python
import functools

import jax
import jax.numpy as jnp
from jax import lax
from jax.experimental import pallas as pl
from jax.experimental.pallas import tpu as pltpu
from jax.sharding import PartitionSpec as P

LOG2E = 1.4426950408889634
NT = (((1,), (1,)), ((), ()))
TN = (((0,), (0,)), ((), ()))


def attend_body(total, unroll, len_ref, qkv_ref, do_ref, ctx_ref, grad_ref, gk_t, gv_t):
    lane = lax.broadcasted_iota(jnp.int32, (128, 128), 1)
    low = lane < 64

    def twice(x):
        zero = jnp.zeros_like(x)
        return jnp.concatenate([jnp.where(low, x, zero), jnp.where(low, zero, x)], axis=0)

    def fold(x):
        return jnp.where(low, x[:128], x[128:])

    def window(span, start, end):
        base = pl.multiple_of(jnp.minimum((start // 16) * 16, total - span), 16)
        key_pos = base + lax.broadcasted_iota(jnp.int32, (1, span), 1)
        bias = jnp.where((key_pos >= start) & (key_pos < end), 0.0, -1e30).astype(jnp.float32)
        gk_t[:, :span] = jnp.zeros((128, span), jnp.float32)
        gv_t[:, :span] = jnp.zeros((128, span), jnp.float32)

        def block(index, _):
            row = pl.multiple_of(base + index * 128, 16)
            rows = pl.ds(row, 128)
            keys = qkv_ref[pl.ds(base, span), 128:256]
            values = qkv_ref[pl.ds(base, span), 256:384]
            row_pos = row + lax.broadcasted_iota(jnp.int32, (128, 128), 0)
            valid = (row_pos >= start) & (row_pos < end)
            query = twice(qkv_ref[rows, 0:128])
            cot = jnp.where(valid, do_ref[rows, :].astype(jnp.float32), 0.0)
            cot = twice(cot)
            s = lax.dot_general(query, keys, NT, preferred_element_type=jnp.float32)
            s = s * (0.125 * LOG2E) + bias
            e = jnp.exp2(s - jnp.max(s, axis=1, keepdims=True))
            inv = 1.0 / jnp.sum(e, axis=1, keepdims=True)
            weights = e.astype(jnp.bfloat16)
            ctx = jnp.dot(weights, values, preferred_element_type=jnp.float32) * inv
            cot_n = cot * inv
            delta = jnp.sum(cot_n * ctx, axis=1, keepdims=True)
            cot_b = cot_n.astype(jnp.bfloat16)
            dp = lax.dot_general(cot_b, values, NT, preferred_element_type=jnp.float32)
            ds = (e * (dp - delta)).astype(jnp.bfloat16)
            gv_t[:, :span] += lax.dot_general(cot_b, weights, TN, preferred_element_type=jnp.float32)
            gk_t[:, :span] += lax.dot_general(query, ds, TN, preferred_element_type=jnp.float32)
            gq = jnp.dot(ds, keys, preferred_element_type=jnp.float32)
            ctx_ref[rows, :] = jnp.where(valid, fold(ctx), ctx_ref[rows, :].astype(jnp.float32)).astype(jnp.bfloat16)
            grad_ref[rows, 0:128] = jnp.where(
                valid, fold(gq) * 0.125, grad_ref[rows, 0:128].astype(jnp.float32)).astype(jnp.bfloat16)
            return 0

        lax.fori_loop(0, span // 128, block, 0, unroll=min(unroll, span // 128) if unroll else True)
        for part in range(span // 128):
            rows = pl.ds(pl.multiple_of(base + part * 128, 16), 128)
            row_pos = base + part * 128 + lax.broadcasted_iota(jnp.int32, (128, 128), 0)
            valid = (row_pos >= start) & (row_pos < end)
            cols = slice(part * 128, part * 128 + 128)
            gk = gk_t[:, cols].T * 0.125
            gv = gv_t[:, cols].T
            grad_ref[rows, 128:256] = jnp.where(
                valid, gk, grad_ref[rows, 128:256].astype(jnp.float32)).astype(jnp.bfloat16)
            grad_ref[rows, 256:384] = jnp.where(
                valid, gv, grad_ref[rows, 256:384].astype(jnp.float32)).astype(jnp.bfloat16)

    def utterance(index, start):
        end = start + len_ref[index]
        tiles = (end - (start // 16) * 16 + 127) // 128
        for count in range(1, 6):
            @pl.when(tiles == count)
            def _():
                window(count * 128, start, end)
        return end

    lax.fori_loop(0, len_ref.shape[0], utterance, jnp.int32(0))


def attend(lengths, qkv, cot, unroll=1):
    total = qkv.shape[0]
    return pl.pallas_call(
        functools.partial(attend_body, total, unroll),
        out_shape=(jax.ShapeDtypeStruct((total, 128), jnp.bfloat16),
                   jax.ShapeDtypeStruct((total, 384), jnp.bfloat16)),
        in_specs=[pl.BlockSpec(memory_space=pltpu.SMEM)] + [pl.BlockSpec(memory_space=pltpu.VMEM)] * 2,
        out_specs=(pl.BlockSpec(memory_space=pltpu.VMEM),) * 2,
        scratch_shapes=[pltpu.VMEM((128, 640), jnp.float32)] * 2,
        compiler_params=pltpu.CompilerParams(vmem_limit_bytes=12 * 2**20),
        name="attention",
    )(lengths, qkv, cot)


MESH = pl.DeviceIdType.MESH
BF = jnp.bfloat16
F32 = jnp.float32


def place():
    f = lax.axis_index("fsdp")
    s = lax.axis_index("seq")
    return f, s


def greet(f, s, ranks, shards):
    barrier = pltpu.get_barrier_semaphore()
    for k in range(1, ranks):
        pl.semaphore_signal(barrier, inc=1, device_id=(f, lax.rem(s + k, ranks)), device_id_type=MESH)
    for k in range(1, shards):
        pl.semaphore_signal(barrier, inc=1, device_id=(lax.rem(f + k, shards), s), device_id_type=MESH)
    pl.semaphore_wait(barrier, ranks + shards - 2)


def whiten(values_in):
    average = jnp.mean(values_in, axis=1, keepdims=True)
    centred = values_in - average
    variance = jnp.mean(centred * centred, axis=1, keepdims=True)
    inverse_scale = lax.rsqrt(variance + 1e-05)
    return centred * inverse_scale, inverse_scale


def front_body(ranks, shards, frames_in, cot_in, w_in, normed, qkv, cot, w, frames,
               cot_send, cot_recv, one_send, one_recv, two_send, two_recv, mate_send, mate_recv, send, recv, local):
    f, s = place()
    rows = frames.shape[0]
    half = rows // 2
    chip, core = s // 2, lax.rem(s, 2)
    chips = ranks // 2
    sides = w.shape[2]
    fy, fz = f // sides, lax.rem(f, sides)
    right = lax.rem(chip + 1, chips) * 2 + core
    left = lax.rem(chip + chips - 1, chips) * 2 + core
    across = lax.rem(chip + 2, chips) * 2 + core
    flip = 1 - 2 * core
    partner = s + flip
    head = pl.ds(pl.multiple_of(s * 128, 128), 128)

    pieces = []
    for i in range(chips):
        for t in range(3):
            column = pl.multiple_of((t * ranks + 2 * i + core) * 128, 128)
            pieces.append(pltpu.make_async_copy(
                w_in.at[:, pl.ds(column, 128)], w.at[i, core, fy, fz, :, pl.ds(t * 128, 128)], local.at[i * 3 + t]))
            pieces[-1].start()
    load_x = pltpu.make_async_copy(frames_in, frames, local.at[3 * chips])
    load_x.start()
    own_cot = pltpu.make_async_copy(
        cot_in.at[:, head], cot.at[pl.ds(pl.multiple_of(s * rows, 128), rows)], local.at[3 * chips + 1])
    own_cot.start()
    greet(f, s, ranks, shards)

    started = []

    def remote(ref, sends, recvs, role, target):
        return pltpu.make_async_remote_copy(
            src_ref=ref, dst_ref=ref, send_sem=sends.at[role], recv_sem=recvs.at[role],
            device_id=target, device_id_type=MESH)

    def push(ref, sends, recvs, role, target):
        copy = remote(ref, sends, recvs, role, target)
        copy.start()
        started.append(copy)

    def block(rank, offset=0, count=rows):
        return normed.at[pl.ds(pl.multiple_of(rank * rows + offset, 64), count)]

    def move(role, rank, offset, count, target):
        push(block(rank, offset, count), send, recv, role, (f, target))

    def arrived(role, rank, offset, count):
        remote(block(rank, offset, count), send, recv, role, (f, s)).wait_recv()

    cots = []
    for k in (4, 3, 5, 2, 6, 1, 7):
        d = lax.rem(s + k, ranks)
        copy = pltpu.make_async_remote_copy(
            src_ref=cot_in.at[:, pl.ds(pl.multiple_of(d * 128, 128), 128)],
            dst_ref=cot.at[pl.ds(pl.multiple_of(s * rows, 128), rows)],
            send_sem=cot_send.at[k], recv_sem=cot_recv.at[k], device_id=(f, d), device_id_type=MESH)
        copy.start()
        cots.append(copy)
    for piece in pieces:
        piece.wait()

    def along(axis, step):
        if axis == 0:
            return lax.rem(fy + step, sides) * sides + fz
        return fy * sides + lax.rem(fz + step, sides)

    def shard(pair, peer):
        return w.at[pl.ds(2 * pair, 2), core, peer // sides, lax.rem(peer, sides)]

    for k in (2, 1, 3):
        for pair in range(2):
            push(shard(pair, f), one_send, one_recv, 4 * pair + k, (along(1 - pair, k), s))

    def norm(offset):
        whitened, _ = whiten(frames[pl.ds(offset, half), :].astype(F32))
        normed[pl.ds(pl.multiple_of(s * rows + offset, 64), half), :] = whitened.astype(BF)

    load_x.wait()
    norm(0)
    move(0, s, 0, half, right)
    norm(half)
    move(2, s, half, half, left)
    move(1, s, half, half, right)
    move(3, s, 0, half, left)
    move(6, s, 0, rows, partner)
    own_cot.wait()

    def line(pair, index, step):
        i = 2 * pair + index
        if pair == 0:
            return w.at[i, core, lax.rem(fy + step, sides)]
        return w.at[i, core, :, lax.rem(fz + step, sides)]

    def pass_on(role, pair, index, step, toward):
        push(line(pair, index, step), two_send, two_recv, 6 * pair + role, (along(pair, toward), s))

    def come(role, pair, index, step):
        remote(line(pair, index, step), two_send, two_recv, 6 * pair + role, (f, s)).wait_recv()

    up, down = 1, sides - 1
    for pair in range(2):
        for k in (1, 3, 2):
            peer = along(1 - pair, sides - k)
            remote(shard(pair, peer), one_send, one_recv, 4 * pair + k, (f, s)).wait_recv()
        pass_on(0, pair, 0, 0, up)
        pass_on(1, pair, 1, 0, down)
        pass_on(2, pair, 1, 0, up)
        pass_on(3, pair, 0, 0, down)
    for pair in range(2):
        come(0, pair, 0, down)
        pass_on(4, pair, 0, down, up)
        come(1, pair, 1, up)
        pass_on(5, pair, 1, up, down)

    arrived(0, left, 0, half)
    move(4, left, 0, half, right)
    arrived(2, right, half, half)
    move(5, right, half, half, left)

    for pair in range(2):
        come(2, pair, 1, down)
        come(3, pair, 0, up)
        come(4, pair, 0, 2)
        come(5, pair, 1, 2)
        push(w.at[pl.ds(2 * pair, 2), core], mate_send, mate_recv, pair, (f, partner))

    mine = s // 2

    def project(rank):
        def tile(i, _):
            at = pl.ds(pl.multiple_of(rank * rows + i * half, 64), half)
            weight = w[mine, core].reshape(w.shape[2] * w.shape[3] * w.shape[4], w.shape[5])
            qkv[at, :] = jnp.dot(normed[at, :], weight, preferred_element_type=F32).astype(BF)
            return 0
        lax.fori_loop(0, 2, tile, 0)

    project(s)
    arrived(6, partner, 0, rows)
    project(partner)
    arrived(1, left, half, half)
    move(7, left, 0, rows, partner)
    arrived(3, right, 0, half)
    move(8, right, 0, rows, partner)
    project(left)
    project(right)
    arrived(7, left + flip, 0, rows)
    project(left + flip)
    arrived(8, right + flip, 0, rows)
    project(right + flip)
    for pair in range(2):
        remote(w.at[pl.ds(2 * pair, 2), 1 - core], mate_send, mate_recv, pair, (f, s)).wait_recv()
    arrived(4, across, 0, half)
    move(9, across, 0, half, partner)
    arrived(5, across, half, half)
    move(10, across, half, half, partner)
    project(across)
    arrived(9, across + flip, 0, half)
    arrived(10, across + flip, half, half)
    project(across + flip)
    for copy in cots:
        copy.wait()
    for copy in started:
        copy.wait_send()


VM = pl.BlockSpec(memory_space=pltpu.VMEM)
HBM = pl.BlockSpec(memory_space=pltpu.HBM)
FRONT_MB = 8
BACK_MB = 22
DMA = pltpu.SemaphoreType.DMA


def front(ranks, shards, frames, cot_in, w_in):
    rows, model = frames.shape
    total = rows * ranks
    sides = 4
    weight = (ranks // 2, 2, sides, shards // sides, w_in.shape[0], 384)
    return pl.pallas_call(
        functools.partial(front_body, ranks, shards),
        out_shape=(jax.ShapeDtypeStruct((total, model), BF), jax.ShapeDtypeStruct((total, 384), BF),
                   jax.ShapeDtypeStruct((total, 128), BF), jax.ShapeDtypeStruct(weight, BF)),
        in_specs=[HBM] * 3,
        out_specs=(VM,) * 4,
        scratch_shapes=[pltpu.VMEM((rows, model), BF),
                        DMA((ranks,)), DMA((ranks,)), DMA((8,)), DMA((8,)), DMA((12,)), DMA((12,)), DMA((2,)), DMA((2,)),
                        DMA((11,)), DMA((11,)), DMA((3 * ranks // 2 + 2,))],
        compiler_params=pltpu.CompilerParams(collective_id=0, has_side_effects=True, vmem_limit_bytes=FRONT_MB * 2**20),
        name="front",
    )(frames, cot_in, w_in)


def back_body(ranks, shards, ctx, grads, frames_in, normed, w, ctx_out, gi_out, gw_out,
              frames, grads_t, got, part, shares, acc, white, scale, total_w,
              g_send, g_recv, c_send, c_recv, r_send, r_recv, p_send, p_recv, local):
    f, s = place()
    rows, model = frames_in.shape
    depth = model // shards
    sides = 4
    fy, fz = f // sides, lax.rem(f, sides)
    load_x = pltpu.make_async_copy(frames_in, frames, local.at[0])
    load_x.start()
    greet(f, s, ranks, shards)
    order = (1, 7, 2, 6, 3, 5, 4)
    sent = {}
    for k in order:
        d = lax.rem(s + k, ranks)
        theirs = pl.ds(pl.multiple_of(d * rows, 128), rows)
        sent[k] = (
            pltpu.make_async_remote_copy(
                src_ref=grads.at[theirs], dst_ref=got.at[k], send_sem=g_send.at[k], recv_sem=g_recv.at[k],
                device_id=(f, d), device_id_type=MESH),
            pltpu.make_async_remote_copy(
                src_ref=ctx.at[theirs], dst_ref=ctx_out.at[:, pl.ds(pl.multiple_of(s * 128, 128), 128)],
                send_sem=c_send.at[k], recv_sem=c_recv.at[k], device_id=(f, d), device_id_type=MESH))
        for copy in sent[k]:
            copy.start()
    mine = pl.ds(pl.multiple_of(s * rows, 128), rows)
    ctx_out[:, pl.ds(pl.multiple_of(s * 128, 128), 128)] = ctx[mine, :]

    def turn(i, _):
        at = pl.ds(pl.multiple_of(i * 128, 128), 128)
        grads_t[:, at] = grads[at, :].T
        return 0

    lax.fori_loop(0, grads.shape[0] // 128, turn, 0)
    group = depth * sides
    shared = []
    for j in (1, 2, 3, 0):
        y = lax.rem(fy + j, sides)
        at = pl.ds(pl.multiple_of(y * group, 128), group)
        product = jnp.dot(grads_t[...], normed[:, at], preferred_element_type=F32)
        part[at, :] = product.T.astype(BF)
        for k in (1, 2, 3, 0):
            if j == 0 and k == 0:
                continue
            peer = y * sides + lax.rem(fz + k, sides)
            copy = pltpu.make_async_remote_copy(
                src_ref=part.at[pl.ds(pl.multiple_of(peer * depth, 32), depth)], dst_ref=shares.at[4 * j + k],
                send_sem=r_send.at[4 * j + k], recv_sem=r_recv.at[4 * j + k],
                device_id=(peer, s), device_id_type=MESH)
            copy.start()
            shared.append(copy)

    def prepare(i, _):
        at = pl.ds(pl.multiple_of(i * depth, 32), depth)
        whitened, inverse_scale = whiten(frames[at, :].astype(F32))
        white[at, :] = whitened
        scale[at, :] = jnp.broadcast_to(inverse_scale, (depth, 128))
        return 0

    load_x.wait()
    lax.fori_loop(0, rows // depth, prepare, 0)

    def pull(block, rank):
        return lax.dot_general(block, w[rank], NT, preferred_element_type=F32)

    acc[...] = pull(grads[mine, :], s)
    for k in order[:4]:
        sent[k][0].wait_recv()
        acc[...] += pull(got[k], lax.rem(s + ranks - k, ranks))
    for copy in shared:
        copy.wait_recv()
    sums = part[pl.ds(pl.multiple_of(f * depth, 32), depth), :].astype(F32)
    for k in range(1, shards):
        sums += shares[k].astype(F32)
    total_w[...] = sums
    for t in range(3):
        number = t * ranks + s
        owner, slot = number // 3, lax.rem(number, 3)
        source = total_w.at[:, pl.ds(t * 128, 128)]
        target = gw_out.at[:, pl.ds(pl.multiple_of(slot * 128, 128), 128)]

        @pl.when(owner != s)
        def _():
            pltpu.make_async_remote_copy(
                src_ref=source, dst_ref=target, send_sem=p_send.at[t], recv_sem=p_recv.at[slot],
                device_id=(f, owner), device_id_type=MESH).start()

        @pl.when(owner == s)
        def _():
            target[...] = sums[:, t * 128:t * 128 + 128]

    for k in order[4:]:
        sent[k][0].wait_recv()
        acc[...] += pull(got[k], lax.rem(s + ranks - k, ranks))

    def finish(i, _):
        at = pl.ds(pl.multiple_of(i * depth, 32), depth)
        gn = acc[at, :]
        whitened = white[at, :]
        inner = jnp.mean(gn * whitened, axis=1, keepdims=True)
        out = scale[at, 0:1] * (gn - jnp.mean(gn, axis=1, keepdims=True) - whitened * inner)
        gi_out[at, :] = out.astype(BF)
        return 0

    lax.fori_loop(0, rows // depth, finish, 0)
    for slot in range(3):
        source_rank = lax.rem(3 * s + slot, ranks)

        @pl.when(source_rank != s)
        def _():
            pltpu.make_async_remote_copy(
                src_ref=total_w.at[:, pl.ds(0, 128)], dst_ref=gw_out.at[:, pl.ds(slot * 128, 128)],
                send_sem=p_send.at[slot], recv_sem=p_recv.at[slot], device_id=(f, s), device_id_type=MESH).wait_recv()

    for t in range(3):
        owner = (t * ranks + s) // 3

        @pl.when(owner != s)
        def _():
            pltpu.make_async_remote_copy(
                src_ref=total_w.at[:, pl.ds(t * 128, 128)], dst_ref=gw_out.at[:, pl.ds(0, 128)],
                send_sem=p_send.at[t], recv_sem=p_recv.at[t], device_id=(f, owner), device_id_type=MESH).wait_send()

    for k in order:
        sent[k][0].wait_send()
        sent[k][1].wait()
    for copy in shared:
        copy.wait_send()


def back(ranks, shards, ctx, grads, frames, normed, w):
    rows, model = frames.shape
    total = rows * ranks
    depth = model // shards
    return pl.pallas_call(
        functools.partial(back_body, ranks, shards),
        out_shape=(jax.ShapeDtypeStruct((rows, ranks * 128), BF), jax.ShapeDtypeStruct((rows, model), BF),
                   jax.ShapeDtypeStruct((depth, 384), F32)),
        in_specs=[VM] * 2 + [HBM] + [VM] * 2,
        out_specs=(VM,) * 3,
        scratch_shapes=[
            pltpu.VMEM((rows, model), BF), pltpu.VMEM((384, total), BF),
            pltpu.VMEM((ranks, rows, 384), BF), pltpu.VMEM((model, 384), BF), pltpu.VMEM((shards, depth, 384), BF),
            pltpu.VMEM((rows, model), F32), pltpu.VMEM((rows, model), F32), pltpu.VMEM((rows, 128), F32),
            pltpu.VMEM((depth, 384), F32)]
        + [DMA((ranks,))] * 4 + [DMA((shards,))] * 2 + [DMA((3,))] * 2 + [DMA((1,))],
        compiler_params=pltpu.CompilerParams(collective_id=1, has_side_effects=True, vmem_limit_bytes=BACK_MB * 2**20),
        name="back",
    )(ctx, grads, frames, normed, w)


def per_device(frames, lengths, w_qkv, d_context):
    ranks, shards = lax.axis_size("seq"), lax.axis_size("fsdp")
    model = frames.shape[2]
    normed, qkv, cot, weight_full = front(ranks, shards, frames[0], d_context[0], w_qkv)
    context, grads = attend(lengths[0], qkv, cot, 5)
    context_out, grad_input, grad_weight = back(
        ranks, shards, context, grads, frames[0], normed, weight_full.reshape(ranks, model, 384))
    return context_out[None], grad_input[None], grad_weight


def solution(mesh):
    return jax.shard_map(
        per_device,
        mesh=mesh,
        in_specs=(P("fsdp", "seq", None), P("fsdp", None), P("fsdp", None), P("fsdp", "seq", None)),
        out_specs=(P("fsdp", "seq", None), P("fsdp", "seq", None), P("fsdp", "seq")),
        check_vma=False,
    )
```
